32 devices in a mesh: grid: 4 (over z), band: 4 (over y, x), atom: 2 (over core).
Axes of the slice: x: 2, y: 2, z: 4, core: 2. Of those that a mesh axis runs over, the one named last changes fastest.
Arguments:
- psi: float32 [256, 64, 1024], P('band', 'grid'), may hold values from -27 to 27
- potential: float32 [64, 1024], P(('grid', 'atom')), may hold values from -12 to 12
- projectors: float32 [128, 4, 512], P('grid'), may hold values from -5 to 5
- strength: float32 [128, 4], P('grid'), may hold values from 0.5 to 8
- sphere_index: int32 [128, 512], P('grid'), may hold values from 2048 to 25599, as said below
- atom_count: int32 [4], P('grid'), may hold values from 2 to 32, as said below
Outputs:
- orthonormal: float32 [256, 64, 1024], P('band', ('grid', 'atom'))
The draws below stay inside these ranges and needn't reach their ends.
Inputs may be any that keep to these rules, and one draw needn't show every extreme that they name: `sphere_index`: row a lists the 512 cells of an 8 x 8 x 8 cube about the atom's centre, offsets -4 to 3 in each direction, as e * 1024 + x * 32 + y with e counted from 6 rows below its domain. `atom_count`: the live slots of a domain are its first ones; in every draw some domain has all 32 live.
All inputs are finite; a program needn't handle non-finite values.
Results may differ from the reference program's by a relative error of at most 0.0003.
Values sent between devices are 32-bit elements; how exact they have to be, the bound alone decides.
A program may use at most 128 MiB of HBM per device.

```python
import math
import jax
import jax.numpy as jnp
from jax import lax

BANDS = 256
PROJ = 4
SPHERE = 512
CX = 32
CY = 32
CZ = 16
ATOM_DOM = 32
NZ = 64
NXY = 1024
CELLS = 65536
ATOMS = 128
N_GRID = 4


def draw_psi(key, part):
    key_own, key_weight, key_common = jax.random.split(key, 3)
    weights = jax.random.uniform(key_weight, (BANDS, 1, 1), jnp.float32, -1.0, 1.0)
    common = jnp.clip(jax.random.normal(key_common, (1, NZ, NXY), jnp.float32), -6.0, 6.0)
    rising = 1.0 + 2.0 * jnp.arange(NZ, dtype=jnp.float32).reshape(1, NZ, 1) / (NZ - 1)
    own_part = jnp.clip(jax.random.normal(key_own, (BANDS, NZ, NXY), jnp.float32), -6.0, 6.0)
    shared = 0.5
    return rising * (own_part + shared * weights * common)


def draw_sphere_index(key, part):
    key_z, key_x, key_y = jax.random.split(key, 3)
    centre_z = jax.random.randint(key_z, (ATOMS,), 0, CZ, jnp.int32)
    centre_x = jax.random.randint(key_x, (ATOMS,), 4, CX - 3, jnp.int32)
    centre_y = jax.random.randint(key_y, (ATOMS,), 4, CY - 3, jnp.int32)
    slot = jnp.arange(ATOMS, dtype=jnp.int32) % ATOM_DOM
    centre_z = jnp.where(slot == 0, CZ - 1, jnp.where(slot == 1, 0, centre_z))
    centre_x = jnp.where(slot == 0, CX - 4, jnp.where(slot == 1, 4, centre_x))
    centre_y = jnp.where(slot == 0, CY - 4, jnp.where(slot == 1, 4, centre_y))
    offsets = jnp.arange(SPHERE, dtype=jnp.int32)
    shift_z = offsets // 64 - 4
    shift_x = offsets // 8 % 8 - 4
    shift_y = offsets % 8 - 4
    rows_ext = centre_z[:, None] + 6 + shift_z[None, :]
    cols_x = centre_x[:, None] + shift_x[None, :]
    cols_y = centre_y[:, None] + shift_y[None, :]
    return (rows_ext * NXY + cols_x * CY + cols_y).astype(jnp.int32)


def draw_atom_count(key, part):
    key_count, key_full = jax.random.split(key)
    counts = jax.random.randint(key_count, (N_GRID,), 2, ATOM_DOM + 1, jnp.int32)
    chosen = jax.random.randint(key_full, (), 0, N_GRID, jnp.int32)
    return jnp.where(jnp.arange(N_GRID, dtype=jnp.int32) == chosen, ATOM_DOM, counts).astype(jnp.int32)


def shard_levels(rng, extent, cuts, least, top_value):
    def one(position, parts):
        steps = jax.random.uniform(jax.random.fold_in(jax.random.fold_in(rng, 6), position), (parts,), jnp.float32, least / len(cuts), top_value / len(cuts))
        return jnp.repeat(jnp.exp(steps), extent[position] // parts).reshape((-1,) + (1,) * (len(extent) - position - 1))

    level = one(*cuts[0])
    for cut in cuts[1:]:
        level = level * one(*cut)
    return level


def normal_values(rng, extent, spread, reach, cuts=(), kind=jnp.bfloat16):
    factor_of = shard_levels(rng, extent, cuts, -0.22, 0.18) if cuts else 1.0
    values = jax.random.normal(rng, extent, jnp.float32) * spread * factor_of
    return jnp.minimum(jnp.maximum(values, -reach), reach).astype(kind)


def setup_inputs(seed: int = 0) -> dict:
    key_of = jax.random.split(jax.random.key(seed), 7)
    psi = draw_psi(jax.random.fold_in(key_of[6], 71), 0)
    potential = normal_values(key_of[1], (NZ, NXY), 3.0, 12.0, ((0, 8),), jnp.float32)
    projectors = normal_values(key_of[2], (ATOMS, PROJ, SPHERE), 1.0, 5.0, ((0, 4),), jnp.float32)
    strength = jnp.clip(jnp.exp(math.log(8.0) - 2.7725887 * jax.random.uniform(key_of[3], (ATOMS, PROJ), jnp.float32) ** shard_levels(key_of[3], (ATOMS, PROJ), ((0, 4),), -0.2, 0.2)), 0.5, 8.0)
    sphere_index = draw_sphere_index(jax.random.fold_in(key_of[6], 71), 0)
    atom_count = draw_atom_count(jax.random.fold_in(key_of[6], 71), 0)
    return {"psi": psi, "potential": potential, "projectors": projectors, "strength": strength, "sphere_index": sphere_index, "atom_count": atom_count}


STENCIL = (-5369.0 / 1800.0, 12.0 / 7.0, -15.0 / 56.0, 10.0 / 189.0, -1.0 / 112.0, 2.0 / 1925.0, -1.0 / 16632.0)
KINETIC = -0.5 * 4.0
STEP_SIZE = 0.05
HIGHEST = lax.Precision.HIGHEST

def laplace_band(band_field):
    padded = jnp.pad(band_field, ((0, 0), (6, 6), (6, 6)))
    accumulated = 3.0 * STENCIL[0] * band_field
    for k in range(1, 7):
        along_z = jnp.roll(band_field, k, 0) + jnp.roll(band_field, -k, 0)
        along_x = padded[:, 6 + k:6 + k + CX, 6:6 + CY] + padded[:, 6 - k:6 - k + CX, 6:6 + CY]
        along_y = padded[:, 6:6 + CX, 6 + k:6 + k + CY] + padded[:, 6:6 + CX, 6 - k:6 - k + CY]
        accumulated = accumulated + STENCIL[k] * (along_z + along_x + along_y)
    return accumulated

def reference(psi, potential, projectors, strength, sphere_index, atom_count):
    atom_rows = jnp.arange(ATOMS, dtype=jnp.int32)
    domain = atom_rows // ATOM_DOM
    ext_rows = sphere_index // NXY
    plane_cell = sphere_index % NXY
    global_z = (domain[:, None] * CZ + ext_rows - 6) % NZ
    cell_index = (global_z * NXY + plane_cell).astype(jnp.int32)
    alive_mask = (atom_rows % ATOM_DOM < atom_count[domain]).astype(jnp.float32)
    scaled = strength * alive_mask[:, None]
    flat_cells = cell_index.reshape(-1)

    def one_band(band_field):
        flattened = band_field.reshape(NZ * NXY)
        points = flattened[cell_index]
        intersections = jnp.einsum('as,ais->ai', points, projectors, precision=HIGHEST) / math.sqrt(SPHERE)
        values = jnp.einsum('ai,ais->as', intersections * scaled, projectors, precision=HIGHEST)
        nonlocal_term = jnp.zeros((NZ * NXY,), jnp.float32).at[flat_cells].add(values.reshape(-1))
        laplace = laplace_band(band_field.reshape(NZ, CX, CY)).reshape(NZ, NXY)
        applied = KINETIC * laplace + potential * band_field + nonlocal_term.reshape(NZ, NXY)
        return band_field - STEP_SIZE * applied
    updated = lax.map(one_band, psi)
    matrix_y = updated.reshape(BANDS, CELLS)
    intersection_matrix = lax.dot_general(matrix_y.astype(jnp.float32), matrix_y.astype(jnp.float32), (((1,), (1,)), ((), ())), precision=HIGHEST, preferred_element_type=jnp.float32) / CELLS
    factor = jnp.linalg.cholesky(intersection_matrix)
    orthonormal = lax.linalg.triangular_solve(factor, matrix_y, left_side=True, lower=True)
    return orthonormal.reshape(BANDS, NZ, NXY)
```

```python
import functools
import math

import jax
import jax.numpy as jnp
from jax import lax
from jax.experimental import pallas as pl
from jax.experimental.pallas import tpu as pltpu
from jax.sharding import PartitionSpec as P

CY = 32


STENCIL = (
    -5369.0 / 1800.0,
    12.0 / 7.0,
    -15.0 / 56.0,
    10.0 / 189.0,
    -1.0 / 112.0,
    2.0 / 1925.0,
    -1.0 / 16632.0,
)
KINETIC = -0.5 * 4.0
STEP_SIZE = 0.05
HIGHEST = lax.Precision.HIGHEST
MESH = pl.DeviceIdType.MESH


def split(x):
    hi = x.astype(jnp.bfloat16)
    return hi, (x - hi.astype(jnp.float32)).astype(jnp.bfloat16)


def mm(a, b, dims=((1,), (0,))):
    return lax.dot_general(a, b, (dims, ((), ())), preferred_element_type=jnp.float32)


def mm3(a, b, dims=((1,), (0,))):
    ah, al = split(a)
    bh, bl = split(b)
    return mm(ah, bh, dims) + (mm(ah, bl, dims) + mm(al, bh, dims))


def device(grid, band, atom):
    return {"grid": grid, "band": band, "atom": atom}


def gram_kernel(
    grids, bands, atoms, scale, y_ref, yq_ref, s_ref, part, inbox, zbox, mine, a_sem, p_sem, z_sem, g_sem
):
    g, b, c = lax.axis_index("grid"), lax.axis_index("band"), lax.axis_index("atom")
    plane = bands * atoms
    me = b * atoms + c
    rows, nb = y_ref.shape[1], y_ref.shape[2]
    size = s_ref.shape[0]
    depth = size // plane

    def plane_peer(k):
        p = lax.rem(me + k, plane)
        return p, device(g, p // atoms, lax.rem(p, atoms))

    barrier = pltpu.get_barrier_semaphore()
    for k in range(1, plane):
        pl.semaphore_signal(barrier, inc=1, device_id=plane_peer(k)[1], device_id_type=MESH)
    for k in range(1, grids):
        pl.semaphore_signal(
            barrier, inc=1, device_id=device(lax.rem(g + k, grids), b, c), device_id_type=MESH
        )
    pl.semaphore_wait(barrier, plane - 1 + grids - 1)

    own = pl.ds(pl.multiple_of(b * nb, nb), nb)
    copies = []
    for k in sorted(range(1, bands), key=lambda v: -v):
        p = lax.rem(b + k, bands)
        copies.append(
            pltpu.make_async_remote_copy(
                src_ref=y_ref.at[p],
                dst_ref=yq_ref.at[:, own, :],
                send_sem=a_sem.at[0, k - 1],
                recv_sem=a_sem.at[1, k - 1],
                device_id=device(g, p, c),
                device_id_type=MESH,
            )
        )
        copies[-1].start()
    yq_ref[:, own, :] = y_ref[b]
    for copy in copies:
        copy.wait()

    s_ref[...] = jnp.zeros_like(s_ref)

    def add(r, carry):
        hi, lo = split(yq_ref[r])
        cross = mm(hi, lo, ((1,), (1,)))
        s_ref[...] += mm(hi, hi, ((1,), (1,))) + (cross + cross.T)
        return carry

    lax.fori_loop(0, rows, add, 0)
    part[...] = (s_ref[...] * scale).reshape(plane, depth, size)

    copies = []
    for k in range(1, plane):
        p, where = plane_peer(k)
        copies.append(
            pltpu.make_async_remote_copy(
                src_ref=part.at[p],
                dst_ref=inbox.at[k - 1],
                send_sem=p_sem.at[0, k - 1],
                recv_sem=p_sem.at[1, k - 1],
                device_id=where,
                device_id_type=MESH,
            )
        )
        copies[-1].start()
    for copy in copies:
        copy.wait()
    total = part[me]
    for k in range(1, plane):
        total = total + inbox[k - 1]
    mine[...] = total
    zbox[g] = total
    copies = []
    for k in range(1, grids):
        copies.append(
            pltpu.make_async_remote_copy(
                src_ref=mine,
                dst_ref=zbox.at[g],
                send_sem=z_sem.at[0, k - 1],
                recv_sem=z_sem.at[1, k - 1],
                device_id=device(lax.rem(g + k, grids), b, c),
                device_id_type=MESH,
            )
        )
        copies[-1].start()
    for copy in copies:
        copy.wait()
    total = zbox[0]
    for k in range(1, grids):
        total = total + zbox[k]
    piece = pl.ds(pl.multiple_of(me * depth, depth), depth)
    mine[...] = total
    copies = []
    for k in range(1, plane):
        copies.append(
            pltpu.make_async_remote_copy(
                src_ref=mine,
                dst_ref=s_ref.at[piece, :],
                send_sem=g_sem.at[0, k - 1],
                recv_sem=g_sem.at[1, k - 1],
                device_id=plane_peer(k)[1],
                device_id_type=MESH,
            )
        )
        copies[-1].start()
    s_ref[piece, :] = total
    for copy in copies:
        copy.wait()


def exchange_and_gram(y4, grids, bands, atoms, cells):
    blocks, rows, nb, width = y4.shape
    size = bands * nb
    plane = bands * atoms
    depth = size // plane
    vmem = pl.BlockSpec(memory_space=pltpu.VMEM)
    return pl.pallas_call(
        functools.partial(gram_kernel, grids, bands, atoms, 1.0 / cells),
        out_shape=(
            jax.ShapeDtypeStruct((rows, size, width), jnp.float32),
            jax.ShapeDtypeStruct((size, size), jnp.float32),
        ),
        in_specs=[vmem],
        out_specs=(vmem, vmem),
        scratch_shapes=[
            pltpu.VMEM((plane, depth, size), jnp.float32),
            pltpu.VMEM((plane - 1, depth, size), jnp.float32),
            pltpu.VMEM((grids, depth, size), jnp.float32),
            pltpu.VMEM((depth, size), jnp.float32),
            pltpu.SemaphoreType.DMA((2, bands - 1)),
            pltpu.SemaphoreType.DMA((2, plane - 1)),
            pltpu.SemaphoreType.DMA((2, grids - 1)),
            pltpu.SemaphoreType.DMA((2, plane - 1)),
        ],
        compiler_params=pltpu.CompilerParams(
            collective_id=0, has_side_effects=True, vmem_limit_bytes=56 << 20
        ),
    )(y4)


def factor_kernel(step, s_ref, x_ref, work):
    size = s_ref.shape[0]
    work[:, :size] = s_ref[...]
    rows = lax.broadcasted_iota(jnp.int32, (size, size), 0)
    cols = lax.broadcasted_iota(jnp.int32, (size, size), 1)
    work[:, size:] = jnp.where(rows == cols, 1.0, 0.0)
    row = lax.broadcasted_iota(jnp.int32, (step, 1), 0)
    eye = jnp.where(
        lax.broadcasted_iota(jnp.int32, (step, step), 0)
        == lax.broadcasted_iota(jnp.int32, (step, step), 1),
        1.0,
        0.0,
    )
    for k in range(size // step):
        lo, hi = k * step, (k + 1) * step
        pair = jnp.concatenate([work[lo:hi, lo:hi], eye], axis=1)
        scales = jnp.zeros((step, 1), jnp.float32)
        for j in range(step):
            line = pair[j : j + 1, :]
            pivot = pair[j : j + 1, j : j + 1]
            column = pair[:, j : j + 1]
            scales = jnp.where(row == j, lax.rsqrt(pivot), scales)
            ratio = jnp.where(row > j, column / pivot, 0.0)
            pair = pair - ratio * line
        inverse = pair[:, step:] * scales
        block = mm6(inverse, work[lo:hi, :])
        x_ref[lo:hi, :] = block[:, size:]
        if hi < size:
            work[hi:, :] = work[hi:, :] - mm6(block[:, hi:size], block, ((0,), (0,)))


def mm6(a, b, dims=((1,), (0,))):
    return lax.dot_general(
        a, b, (dims, ((), ())), precision=HIGHEST, preferred_element_type=jnp.float32
    )


def inverse_factor(s, step):
    size = s.shape[0]
    vmem = pl.BlockSpec(memory_space=pltpu.VMEM)
    return pl.pallas_call(
        functools.partial(factor_kernel, step),
        out_shape=jax.ShapeDtypeStruct((size, size), jnp.float32),
        in_specs=[vmem],
        out_specs=vmem,
        scratch_shapes=[pltpu.VMEM((size, 2 * size), jnp.float32)],
    )(s)


def combine_kernel(bands, x_ref, yq_ref, o_ref, z, s_sem, r_sem):
    g, b, c = lax.axis_index("grid"), lax.axis_index("band"), lax.axis_index("atom")
    rows, size, width = yq_ref.shape
    nb = size // bands
    barrier = pltpu.get_barrier_semaphore()
    for k in range(1, bands):
        pl.semaphore_signal(
            barrier, inc=1, device_id=device(g, lax.rem(b + k, bands), c), device_id_type=MESH
        )
    pl.semaphore_wait(barrier, bands - 1)
    copies = []
    for r in range(rows):
        z[r] = mm3(x_ref[...], yq_ref[r])
        for k in range(1, bands):
            p = lax.rem(b + k, bands)
            copies.append(
                pltpu.make_async_remote_copy(
                    src_ref=z.at[r, pl.ds(pl.multiple_of(p * nb, nb), nb), :],
                    dst_ref=o_ref.at[b, r],
                    send_sem=s_sem.at[r, k - 1],
                    recv_sem=r_sem.at[r, k - 1],
                    device_id=device(g, p, c),
                    device_id_type=MESH,
                )
            )
            copies[-1].start()
    o_ref[b] = z[:, pl.ds(pl.multiple_of(b * nb, nb), nb), :]
    for copy in copies:
        copy.wait()


def combine_and_return(x, yq, bands):
    rows, size, width = yq.shape
    vmem = pl.BlockSpec(memory_space=pltpu.VMEM)
    return pl.pallas_call(
        functools.partial(combine_kernel, bands),
        out_shape=jax.ShapeDtypeStruct((bands, rows, size // bands, width), jnp.float32),
        in_specs=[vmem, vmem],
        out_specs=vmem,
        scratch_shapes=[
            pltpu.VMEM((rows, size, width), jnp.float32),
            pltpu.SemaphoreType.DMA((rows, bands - 1)),
            pltpu.SemaphoreType.DMA((rows, bands - 1)),
        ],
        compiler_params=pltpu.CompilerParams(
            collective_id=1, has_side_effects=True, vmem_limit_bytes=56 << 20
        ),
    )(x, yq)


def from_behind(block, axis, distance):
    devices = range(lax.axis_size(axis))
    route = [((i - distance) % len(devices), i) for i in devices]
    return lax.ppermute(block, axis, route)


def extended_2(x, sides, width):
    for axis, dim in sides:
        count, length = (lax.axis_size(axis), x.shape[dim])
        up = [(i, (i + 1) % count) for i in range(count)]
        down = [(j, i) for i, j in up]
        last = lax.slice_in_dim(x, length - width, length, axis=dim)
        first = lax.slice_in_dim(x, 0, width, axis=dim)
        before = lax.ppermute(last, axis, up)
        after = lax.ppermute(first, axis, down)
        x = jnp.concatenate([before, x, after], axis=dim)
    return x


def spread_terms(weighted, projectors, sphere_index, total_cells):
    band_rows = weighted.shape[0]
    values = jnp.einsum("nai,ais->nas", weighted, projectors, precision=HIGHEST)
    dense = jnp.zeros((band_rows, total_cells), jnp.float32)
    return dense.at[:, sphere_index.reshape(-1)].add(values.reshape(band_rows, -1))


def fold_rims(dense, depth):
    from_below = from_behind(dense[:, depth + 6 :], "grid", 1)
    from_above = from_behind(dense[:, :6], "grid", -1)
    inner = dense[:, 6 : depth + 6]
    inner = inner.at[:, :6].add(from_below)
    return inner.at[:, depth - 6 :].add(from_above)


def body(psi, potential, projectors, strength, sphere_index, atom_count):
    band_rows, depth, plane_cells = psi.shape
    groups = lax.axis_size("atom")
    core = lax.axis_index("atom")
    half = depth // groups
    extended = extended_2(psi, (("grid", 1),), 6)
    window = lax.dynamic_slice_in_dim(extended, core * half, half + 12, 1)
    centre = window[:, 6 : 6 + half]
    margin = 6 * CY
    padded = jnp.pad(centre, ((0, 0), (0, 0), (margin, margin)))
    column = lax.iota(jnp.int32, plane_cells) % CY
    laplace = 3.0 * STENCIL[0] * centre
    for k in range(1, 7):
        along_z = window[:, 6 + k : 6 + k + half] + window[:, 6 - k : 6 - k + half]
        along_x = (
            padded[:, :, margin + k * CY : margin + k * CY + plane_cells]
            + padded[:, :, margin - k * CY : margin - k * CY + plane_cells]
        )
        upper = jnp.where(column + k < CY, padded[:, :, margin + k : margin + k + plane_cells], 0.0)
        lower = jnp.where(column >= k, padded[:, :, margin - k : margin - k + plane_cells], 0.0)
        laplace = laplace + STENCIL[k] * (along_z + along_x + upper + lower)
    atom_slots = sphere_index.shape[0]
    share = atom_slots // groups
    alive_mask = (lax.iota(jnp.int32, atom_slots) < atom_count[0]).astype(jnp.float32)
    scaled = strength * alive_mask[:, None]
    flattened = extended.reshape(band_rows, -1)
    total_cells = flattened.shape[1]
    own_index = lax.dynamic_slice_in_dim(sphere_index, core * share, share, 0)
    own_projectors = lax.dynamic_slice_in_dim(projectors, core * share, share, 0)
    own_scaled = lax.dynamic_slice_in_dim(scaled, core * share, share, 0)
    points = flattened[:, own_index]
    intersections = jnp.einsum(
        "nas,ais->nai", points, own_projectors, precision=HIGHEST
    ) / math.sqrt(projectors.shape[2])
    weighted = intersections * own_scaled[None]
    dense = spread_terms(weighted, own_projectors, own_index, total_cells).reshape(
        band_rows, depth + 12, plane_cells
    )
    nonlocal_half = lax.psum_scatter(
        fold_rims(dense, depth), "atom", scatter_dimension=1, tiled=True
    )
    updated = centre - STEP_SIZE * (KINETIC * laplace + potential * centre + nonlocal_half)
    grids, bands = lax.axis_size("grid"), lax.axis_size("band")
    cells_total = grids * depth * plane_cells
    width = plane_cells // bands
    y4 = updated.reshape(band_rows, half, bands, width).transpose(2, 1, 0, 3)
    gathered, intersection_matrix = exchange_and_gram(y4, grids, bands, groups, cells_total)
    inverse = inverse_factor(intersection_matrix, band_rows)
    pieces = combine_and_return(inverse, gathered, bands)
    return pieces.transpose(2, 1, 0, 3).reshape(band_rows, half, plane_cells)


def solution(mesh):
    in_specs = (
        P("band", "grid", None),
        P(("grid", "atom"), None),
        P("grid", None, None),
        P("grid", None),
        P("grid", None),
        P("grid"),
    )
    out_specs = P("band", ("grid", "atom"), None)
    return jax.shard_map(body, mesh=mesh, in_specs=in_specs, out_specs=out_specs, check_vma=False)
```

```python
import functools
import math

import jax
import jax.numpy as jnp
from jax import lax
from jax.experimental import pallas as pl
from jax.experimental.pallas import tpu as pltpu
from jax.sharding import PartitionSpec as P

CY = 32


STENCIL = (
    -5369.0 / 1800.0,
    12.0 / 7.0,
    -15.0 / 56.0,
    10.0 / 189.0,
    -1.0 / 112.0,
    2.0 / 1925.0,
    -1.0 / 16632.0,
)
KINETIC = -0.5 * 4.0
STEP_SIZE = 0.05
HIGHEST = lax.Precision.HIGHEST
MESH = pl.DeviceIdType.MESH


def split(x):
    hi = x.astype(jnp.bfloat16)
    return hi, (x - hi.astype(jnp.float32)).astype(jnp.bfloat16)


def mm(a, b, dims=((1,), (0,))):
    return lax.dot_general(a, b, (dims, ((), ())), preferred_element_type=jnp.float32)


def mm3(a, b, dims=((1,), (0,))):
    ah, al = split(a)
    bh, bl = split(b)
    return mm(ah, bh, dims) + (mm(ah, bl, dims) + mm(al, bh, dims))


def device(grid, band, atom):
    return {"grid": grid, "band": band, "atom": atom}


def gram_kernel(
    grids, bands, atoms, scale, y_ref, yq_ref, s_ref, part, inbox, zbox, mine, a_sem, p_sem, z_sem, g_sem
):
    g, b, c = lax.axis_index("grid"), lax.axis_index("band"), lax.axis_index("atom")
    plane = bands * atoms
    me = b * atoms + c
    rows, nb = y_ref.shape[1], y_ref.shape[2]
    size = s_ref.shape[0]
    depth = size // plane

    def plane_peer(k):
        p = lax.rem(me + k, plane)
        return p, device(g, p // atoms, lax.rem(p, atoms))

    barrier = pltpu.get_barrier_semaphore()
    for k in range(1, plane):
        pl.semaphore_signal(barrier, inc=1, device_id=plane_peer(k)[1], device_id_type=MESH)
    for k in range(1, grids):
        pl.semaphore_signal(
            barrier, inc=1, device_id=device(lax.rem(g + k, grids), b, c), device_id_type=MESH
        )
    pl.semaphore_wait(barrier, plane - 1 + grids - 1)

    own = pl.ds(pl.multiple_of(b * nb, nb), nb)
    copies = []
    for k in sorted(range(1, bands), key=lambda v: -v):
        p = lax.rem(b + k, bands)
        copies.append(
            pltpu.make_async_remote_copy(
                src_ref=y_ref.at[p],
                dst_ref=yq_ref.at[:, own, :],
                send_sem=a_sem.at[0, k - 1],
                recv_sem=a_sem.at[1, k - 1],
                device_id=device(g, p, c),
                device_id_type=MESH,
            )
        )
        copies[-1].start()
    yq_ref[:, own, :] = y_ref[b]
    for copy in copies:
        copy.wait()

    s_ref[...] = jnp.zeros_like(s_ref)

    def add(r, carry):
        hi, lo = split(yq_ref[r])
        cross = mm(hi, lo, ((1,), (1,)))
        s_ref[...] += mm(hi, hi, ((1,), (1,))) + (cross + cross.T)
        return carry

    lax.fori_loop(0, rows, add, 0)
    part[...] = (s_ref[...] * scale).reshape(plane, depth, size)

    copies = []
    for k in range(1, plane):
        p, where = plane_peer(k)
        copies.append(
            pltpu.make_async_remote_copy(
                src_ref=part.at[p],
                dst_ref=inbox.at[k - 1],
                send_sem=p_sem.at[0, k - 1],
                recv_sem=p_sem.at[1, k - 1],
                device_id=where,
                device_id_type=MESH,
            )
        )
        copies[-1].start()
    for copy in copies:
        copy.wait()
    total = part[me]
    for k in range(1, plane):
        total = total + inbox[k - 1]
    mine[...] = total
    zbox[g] = total
    copies = []
    for k in range(1, grids):
        copies.append(
            pltpu.make_async_remote_copy(
                src_ref=mine,
                dst_ref=zbox.at[g],
                send_sem=z_sem.at[0, k - 1],
                recv_sem=z_sem.at[1, k - 1],
                device_id=device(lax.rem(g + k, grids), b, c),
                device_id_type=MESH,
            )
        )
        copies[-1].start()
    for copy in copies:
        copy.wait()
    total = zbox[0]
    for k in range(1, grids):
        total = total + zbox[k]
    piece = pl.ds(pl.multiple_of(me * depth, depth), depth)
    mine[...] = total
    copies = []
    for k in range(1, plane):
        copies.append(
            pltpu.make_async_remote_copy(
                src_ref=mine,
                dst_ref=s_ref.at[piece, :],
                send_sem=g_sem.at[0, k - 1],
                recv_sem=g_sem.at[1, k - 1],
                device_id=plane_peer(k)[1],
                device_id_type=MESH,
            )
        )
        copies[-1].start()
    s_ref[piece, :] = total
    for copy in copies:
        copy.wait()


def exchange_and_gram(y4, grids, bands, atoms, cells):
    blocks, rows, nb, width = y4.shape
    size = bands * nb
    plane = bands * atoms
    depth = size // plane
    vmem = pl.BlockSpec(memory_space=pltpu.VMEM)
    return pl.pallas_call(
        functools.partial(gram_kernel, grids, bands, atoms, 1.0 / cells),
        out_shape=(
            jax.ShapeDtypeStruct((rows, size, width), jnp.float32),
            jax.ShapeDtypeStruct((size, size), jnp.float32),
        ),
        in_specs=[vmem],
        out_specs=(vmem, vmem),
        scratch_shapes=[
            pltpu.VMEM((plane, depth, size), jnp.float32),
            pltpu.VMEM((plane - 1, depth, size), jnp.float32),
            pltpu.VMEM((grids, depth, size), jnp.float32),
            pltpu.VMEM((depth, size), jnp.float32),
            pltpu.SemaphoreType.DMA((2, bands - 1)),
            pltpu.SemaphoreType.DMA((2, plane - 1)),
            pltpu.SemaphoreType.DMA((2, grids - 1)),
            pltpu.SemaphoreType.DMA((2, plane - 1)),
        ],
        compiler_params=pltpu.CompilerParams(
            collective_id=0, has_side_effects=True, vmem_limit_bytes=56 << 20
        ),
    )(y4)


def factor_kernel(step, s_ref, x_ref, work):
    size = s_ref.shape[0]
    work[:, :size] = s_ref[...]
    rows = lax.broadcasted_iota(jnp.int32, (size, size), 0)
    cols = lax.broadcasted_iota(jnp.int32, (size, size), 1)
    work[:, size:] = jnp.where(rows == cols, 1.0, 0.0)
    row = lax.broadcasted_iota(jnp.int32, (step, 1), 0)
    eye = jnp.where(
        lax.broadcasted_iota(jnp.int32, (step, step), 0)
        == lax.broadcasted_iota(jnp.int32, (step, step), 1),
        1.0,
        0.0,
    )
    for k in range(size // step):
        lo, hi = k * step, (k + 1) * step
        pair = jnp.concatenate([work[lo:hi, lo:hi], eye], axis=1)
        scales = jnp.zeros((step, 1), jnp.float32)
        for j in range(step):
            line = pair[j : j + 1, :]
            pivot = pair[j : j + 1, j : j + 1]
            column = pair[:, j : j + 1]
            scales = jnp.where(row == j, lax.rsqrt(pivot), scales)
            ratio = jnp.where(row > j, column / pivot, 0.0)
            pair = pair - ratio * line
        inverse = pair[:, step:] * scales
        block = mm6(inverse, work[lo:hi, :])
        x_ref[lo:hi, :] = block[:, size:]
        if hi < size:
            work[hi:, :] = work[hi:, :] - mm6(block[:, hi:size], block, ((0,), (0,)))


def mm6(a, b, dims=((1,), (0,))):
    return lax.dot_general(
        a, b, (dims, ((), ())), precision=HIGHEST, preferred_element_type=jnp.float32
    )


def inverse_factor(s, step):
    size = s.shape[0]
    vmem = pl.BlockSpec(memory_space=pltpu.VMEM)
    return pl.pallas_call(
        functools.partial(factor_kernel, step),
        out_shape=jax.ShapeDtypeStruct((size, size), jnp.float32),
        in_specs=[vmem],
        out_specs=vmem,
        scratch_shapes=[pltpu.VMEM((size, 2 * size), jnp.float32)],
    )(s)


def combine_kernel(bands, x_ref, yq_ref, o_ref, z, s_sem, r_sem):
    g, b, c = lax.axis_index("grid"), lax.axis_index("band"), lax.axis_index("atom")
    rows, size, width = yq_ref.shape
    nb = size // bands
    barrier = pltpu.get_barrier_semaphore()
    for k in range(1, bands):
        pl.semaphore_signal(
            barrier, inc=1, device_id=device(g, lax.rem(b + k, bands), c), device_id_type=MESH
        )
    pl.semaphore_wait(barrier, bands - 1)
    copies = []
    for r in range(rows):
        z[r] = mm3(x_ref[...], yq_ref[r])
        for k in range(1, bands):
            p = lax.rem(b + k, bands)
            copies.append(
                pltpu.make_async_remote_copy(
                    src_ref=z.at[r, pl.ds(pl.multiple_of(p * nb, nb), nb), :],
                    dst_ref=o_ref.at[b, r],
                    send_sem=s_sem.at[r, k - 1],
                    recv_sem=r_sem.at[r, k - 1],
                    device_id=device(g, p, c),
                    device_id_type=MESH,
                )
            )
            copies[-1].start()
    o_ref[b] = z[:, pl.ds(pl.multiple_of(b * nb, nb), nb), :]
    for copy in copies:
        copy.wait()


def combine_and_return(x, yq, bands):
    rows, size, width = yq.shape
    vmem = pl.BlockSpec(memory_space=pltpu.VMEM)
    return pl.pallas_call(
        functools.partial(combine_kernel, bands),
        out_shape=jax.ShapeDtypeStruct((bands, rows, size // bands, width), jnp.float32),
        in_specs=[vmem, vmem],
        out_specs=vmem,
        scratch_shapes=[
            pltpu.VMEM((rows, size, width), jnp.float32),
            pltpu.SemaphoreType.DMA((rows, bands - 1)),
            pltpu.SemaphoreType.DMA((rows, bands - 1)),
        ],
        compiler_params=pltpu.CompilerParams(
            collective_id=1, has_side_effects=True, vmem_limit_bytes=56 << 20
        ),
    )(x, yq)


def plane_kernel(core_rows, rows_ref, potential_ref, base_ref, weights):
    depth, nb, cells = rows_ref.shape
    half = base_ref.shape[0]
    tile = weights.shape[1]
    reach = tile // CY
    shape = weights.shape
    source = lax.broadcasted_iota(jnp.int32, shape, 0) - tile
    target = lax.broadcasted_iota(jnp.int32, shape, 1)
    dx = jnp.abs((source + tile) // CY - reach - target // CY)
    dy = jnp.abs((source + tile) % CY - target % CY)
    value = jnp.zeros(shape, jnp.float32)
    for k in range(1, 7):
        hit = ((dx == k) & (dy == 0)) | ((dx == 0) & (dy == k))
        value = jnp.where(hit, STENCIL[k], value)
    weights[...] = value
    first = lax.axis_index("atom") * core_rows

    def one(k, carry):
        for t in range(cells // tile):
            here = slice(t * tile, (t + 1) * tile)
            low, high = max(t - 1, 0), min(t + 2, cells // tile)
            field = rows_ref[first + k, :, low * tile : high * tile]
            band = weights[(low - t + 1) * tile : (high - t + 1) * tile, :]
            plane = mm3(field, band)
            centre = rows_ref[first + k, :, here]
            applied = KINETIC * (3.0 * STENCIL[0] * centre + plane)
            applied = applied + potential_ref[pl.ds(k, 1), here] * centre
            base_ref[k, :, here] = centre - STEP_SIZE * applied
        return carry

    lax.fori_loop(0, half, one, 0)


def plane_part(rows, potential):
    depth, nb, cells = rows.shape
    half = potential.shape[0]
    vmem = pl.BlockSpec(memory_space=pltpu.VMEM)
    tile = 8 * CY
    return pl.pallas_call(
        functools.partial(plane_kernel, half),
        out_shape=jax.ShapeDtypeStruct((half, nb, cells), jnp.float32),
        in_specs=[vmem, vmem],
        out_specs=vmem,
        scratch_shapes=[pltpu.VMEM((3 * tile, tile), jnp.float32)],
        compiler_params=pltpu.CompilerParams(vmem_limit_bytes=56 << 20),
        cost_estimate=pl.CostEstimate(
            flops=12 * half * nb * cells * tile, bytes_accessed=40 * nb * half * cells, transcendentals=0
        ),
    )(rows, potential)


def dense_kernel(
    extra, table_ref, cubes_ref, rows_ref, sums_ref, near_hi, near_lo, rim_hi, rim_lo, dense
):
    core = lax.axis_index("atom")
    half, projectors, cells = near_hi.shape
    depth = rows_ref.shape[0]
    window = depth + extra
    atoms = table_ref.shape[1]
    each = projectors // atoms
    planes = cubes_ref.shape[1] // each

    def clear(w, carry):
        dense[w] = jnp.zeros((projectors, cells), jnp.float32)
        return carry

    lax.fori_loop(0, window, clear, 0)
    pair = 8 // each

    def build(p, carry):
        for h in range(pair):
            atom = p * pair + h

            @pl.when(table_ref[2, atom] > 0)
            def _():
                cube = cubes_ref[atom]
                rest = jnp.zeros((cube.shape[0], cells - cube.shape[1]), jnp.float32)
                moved = pltpu.roll(jnp.concatenate([cube, rest], axis=1), table_ref[1, atom], 1)
                start = table_ref[0, atom]
                group = dense.at[:, pl.ds(pl.multiple_of(p * 8, 8), 8), :]
                for e in range(planes):
                    group[start + e, h * each : (h + 1) * each, :] = moved[
                        e * each : (e + 1) * each, :
                    ]

        return carry

    lax.fori_loop(0, atoms // pair, build, 0)
    ahead = extra * (1 - core)
    sums_ref[...] = jnp.zeros_like(sums_ref)

    def gather(r, carry):
        sums_ref[...] += mm3(rows_ref[r], dense[r + ahead], ((1,), (1,)))
        return carry

    lax.fori_loop(0, depth, gather, 0)
    own = extra + (half - extra) * core

    def keep_near(k, carry):
        near_hi[k], near_lo[k] = split(dense[own + k])
        return carry

    def keep_rim(k, carry):
        rim_hi[k], rim_lo[k] = split(dense[depth * core + k])
        return carry

    lax.fori_loop(0, half, keep_near, 0)
    lax.fori_loop(0, extra, keep_rim, 0)


def dense_projectors(table, cubes, rows, half, extra, each):
    depth, nb, cells = rows.shape
    projectors = table.shape[1] * each
    vmem = pl.BlockSpec(memory_space=pltpu.VMEM)
    near = jax.ShapeDtypeStruct((half, projectors, cells), jnp.bfloat16)
    rim = jax.ShapeDtypeStruct((extra, projectors, cells), jnp.bfloat16)
    return pl.pallas_call(
        functools.partial(dense_kernel, extra),
        out_shape=(jax.ShapeDtypeStruct((nb, projectors), jnp.float32), near, near, rim, rim),
        in_specs=[pl.BlockSpec(memory_space=pltpu.SMEM), vmem, vmem],
        out_specs=(vmem,) * 5,
        scratch_shapes=[pltpu.VMEM((depth + extra, projectors, cells), jnp.float32)],
        compiler_params=pltpu.CompilerParams(vmem_limit_bytes=60 << 20),
        cost_estimate=pl.CostEstimate(
            flops=6 * depth * nb * cells * projectors,
            bytes_accessed=4 * (depth + half) * projectors * cells,
            transcendentals=0,
        ),
    )(table, cubes, rows)


def update_kernel(
    halo_ref, base_ref, rows_ref, sums_ref, scale_ref, near_hi, near_lo, rim_hi, rim_lo, y_ref, window
):
    core = lax.axis_index("atom")
    extra, nb, cells = halo_ref.shape
    depth = rows_ref.shape[0]
    half = base_ref.shape[0]
    blocks, width = y_ref.shape[0], y_ref.shape[3]
    ahead = extra * (1 - core)

    def put_rows(r, carry):
        window[r + ahead] = rows_ref[r]
        return carry

    def put_halo(k, carry):
        window[depth * core + k] = halo_ref[k]
        return carry

    lax.fori_loop(0, depth, put_rows, 0)
    lax.fori_loop(0, extra, put_halo, 0)

    def gather(k, total):
        hi, lo = split(halo_ref[k])
        dims = ((1,), (1,))
        return total + mm(hi, rim_hi[k], dims) + mm(lo, rim_hi[k], dims) + mm(hi, rim_lo[k], dims)

    total = lax.fori_loop(0, extra, gather, sums_ref[...])
    hi, lo = split(total * scale_ref[...])
    own = extra + (half - extra) * core

    def one(k, carry):
        nonlocal_row = mm(hi, near_hi[k]) + mm(lo, near_hi[k]) + mm(hi, near_lo[k])
        row = base_ref[k] - STEP_SIZE * nonlocal_row
        for d in range(1, 7):
            pair = window[own + k + d] + window[own + k - d]
            row = row - (STEP_SIZE * KINETIC * STENCIL[d]) * pair
        for b in range(blocks):
            y_ref[b, k] = row[:, b * width : (b + 1) * width]
        return carry

    lax.fori_loop(0, half, one, 0)


def update(halo, base, rows, sums, scale, near_hi, near_lo, rim_hi, rim_lo, blocks):
    extra, nb, cells = halo.shape
    half, depth = base.shape[0], rows.shape[0]
    vmem = pl.BlockSpec(memory_space=pltpu.VMEM)
    return pl.pallas_call(
        update_kernel,
        out_shape=jax.ShapeDtypeStruct((blocks, half, nb, cells // blocks), jnp.float32),
        in_specs=[vmem] * 9,
        out_specs=vmem,
        scratch_shapes=[pltpu.VMEM((depth + extra, nb, cells), jnp.float32)],
        compiler_params=pltpu.CompilerParams(vmem_limit_bytes=56 << 20),
    )(halo, base, rows, sums, scale, near_hi, near_lo, rim_hi, rim_lo)


def in_cube_order(projectors, sphere_index, edge, plane_cells):
    cell = lax.iota(jnp.int32, edge * edge * edge)
    offset = cell // (edge * edge) * plane_cells + cell // edge % edge * CY + cell % edge
    first = jnp.min(sphere_index, axis=1, keepdims=True)
    ordered = jnp.all(sphere_index == first + offset[None])

    def arrange(values):
        order = jnp.argsort(sphere_index, axis=1)
        return jnp.take_along_axis(values, order[:, None, :], axis=2)

    return lax.cond(ordered, lambda values: values, arrange, projectors), first[:, 0]


def body(psi, potential, projectors, strength, sphere_index, atom_count):
    band_rows, depth, plane_cells = psi.shape
    groups, grids, bands = (lax.axis_size(name) for name in ("atom", "grid", "band"))
    core = lax.axis_index("atom")
    half = depth // groups
    atom_slots, each, points = projectors.shape
    edge = round(points ** (1 / 3))
    extra = edge - 1
    route = []
    for i in range(grids):
        route.append((i * groups + 1, (i + 1) % grids * groups))
        route.append((i * groups, (i - 1) % grids * groups + 1))

    ordered, first = in_cube_order(projectors, sphere_index, edge, plane_cells)
    alive_mask = (lax.iota(jnp.int32, atom_slots) < atom_count[0]).astype(jnp.float32)
    scaled = strength * alive_mask[:, None] / math.sqrt(points)
    count = atom_slots * each
    lines = -(-count // points)
    scaled_line = jnp.pad(scaled.reshape(-1), (0, lines * points - count)).reshape(lines, points)
    first_line = jnp.pad(first.astype(jnp.float32), (0, points - atom_slots))[None]
    sent = jnp.concatenate([ordered.reshape(count, points), scaled_line, first_line], axis=0)
    got = lax.ppermute(sent, ("grid", "atom"), route)
    edge_rows = lax.dynamic_slice_in_dim(psi, core * (depth - extra), extra, 1).transpose(1, 0, 2)
    halo = lax.ppermute(edge_rows, ("grid", "atom"), route)

    rows = psi.transpose(1, 0, 2)
    base = plane_part(rows, potential)
    other_first = got[-1, :atom_slots].astype(jnp.int32)
    other_scaled = got[count : count + lines].reshape(-1)[:count]
    bottom = jnp.concatenate(
        [first // plane_cells - 6, other_first // plane_cells - 6 + depth * (2 * core - 1)]
    )
    lane = jnp.concatenate([first % plane_cells, other_first % plane_cells])
    touches = (bottom < half * (core + 1)) & (bottom + edge > half * core)
    start = jnp.clip(bottom + extra * (1 - core), 0, depth + extra - edge)
    table = jnp.stack([start, lane, touches.astype(jnp.int32)])
    cubes = jnp.stack([ordered.reshape(count, points), got[:count]])
    cubes = cubes.reshape(2 * atom_slots, each, edge, edge, edge).transpose(0, 2, 1, 3, 4)
    cubes = jnp.pad(cubes, ((0, 0), (0, 0), (0, 0), (0, 0), (0, CY - edge)))
    cubes = cubes.reshape(2 * atom_slots, edge * each, edge * CY)
    dense = dense_projectors(table, cubes, rows, half, extra, each)
    scale = jnp.concatenate([scaled.reshape(-1), other_scaled])[None]
    y4 = update(halo, base, rows, dense[0], scale, *dense[1:], bands)

    cells_total = grids * depth * plane_cells
    gathered, intersection_matrix = exchange_and_gram(y4, grids, bands, groups, cells_total)
    inverse = inverse_factor(intersection_matrix, band_rows)
    pieces = combine_and_return(inverse, gathered, bands)
    return pieces.transpose(2, 1, 0, 3).reshape(band_rows, half, plane_cells)


def solution(mesh):
    in_specs = (
        P("band", "grid", None),
        P(("grid", "atom"), None),
        P("grid", None, None),
        P("grid", None),
        P("grid", None),
        P("grid"),
    )
    out_specs = P("band", ("grid", "atom"), None)
    return jax.shard_map(body, mesh=mesh, in_specs=in_specs, out_specs=out_specs, check_vma=False)
```

```python
import functools
import math

import jax
import jax.numpy as jnp
from jax import lax
from jax.experimental import pallas as pl
from jax.experimental.pallas import tpu as pltpu
from jax.sharding import PartitionSpec as P

CY = 32


STENCIL = (
    -5369.0 / 1800.0,
    12.0 / 7.0,
    -15.0 / 56.0,
    10.0 / 189.0,
    -1.0 / 112.0,
    2.0 / 1925.0,
    -1.0 / 16632.0,
)
KINETIC = -0.5 * 4.0
STEP_SIZE = 0.05
HIGHEST = lax.Precision.HIGHEST
MESH = pl.DeviceIdType.MESH


def split(x):
    hi = x.astype(jnp.bfloat16)
    return hi, (x - hi.astype(jnp.float32)).astype(jnp.bfloat16)


def mm(a, b, dims=((1,), (0,))):
    return lax.dot_general(a, b, (dims, ((), ())), preferred_element_type=jnp.float32)


def mm3(a, b, dims=((1,), (0,))):
    ah, al = split(a)
    bh, bl = split(b)
    return mm(ah, bh, dims) + (mm(ah, bl, dims) + mm(al, bh, dims))


def device(grid, band, atom):
    return {"grid": grid, "band": band, "atom": atom}


def gram_kernel(
    grids, bands, atoms, scale, halo_ref, base_ref, rows_ref, sums_ref, scale_ref, near_hi_ref,
    near_lo_ref, rim_hi_ref, rim_lo_ref, yq_ref, s_ref, window, near_hi, near_lo, rim_hi, rim_lo,
    y_ref, part, inbox, zbox, mine, d_sem, n_sem, a_sem, p_sem, z_sem, g_sem,
):
    g, b, c = lax.axis_index("grid"), lax.axis_index("band"), lax.axis_index("atom")
    plane = bands * atoms
    me = b * atoms + c
    half, nb, width = y_ref.shape[1:]
    size = s_ref.shape[0]
    share = size // plane
    extra, depth = rim_hi.shape[0], window.shape[0] - rim_hi.shape[0]

    loads = [
        pltpu.make_async_copy(rim_hi_ref, rim_hi, d_sem.at[0]),
        pltpu.make_async_copy(rim_lo_ref, rim_lo, d_sem.at[1]),
        pltpu.make_async_copy(halo_ref, window.at[pl.ds(depth * c, extra)], d_sem.at[2]),
        pltpu.make_async_copy(rows_ref, window.at[pl.ds(extra * (1 - c), depth)], d_sem.at[3]),
    ]
    for load in loads:
        load.start()

    def near_loads(k):
        return (
            pltpu.make_async_copy(near_hi_ref.at[k], near_hi.at[k], n_sem.at[0, k]),
            pltpu.make_async_copy(near_lo_ref.at[k], near_lo.at[k], n_sem.at[1, k]),
        )

    def start_near(k, carry):
        for load in near_loads(k):
            load.start()
        return carry

    lax.fori_loop(0, half, start_near, 0)

    def plane_peer(k):
        p = lax.rem(me + k, plane)
        return p, device(g, p // atoms, lax.rem(p, atoms))

    barrier = pltpu.get_barrier_semaphore()
    for k in range(1, plane):
        pl.semaphore_signal(barrier, inc=1, device_id=plane_peer(k)[1], device_id_type=MESH)
    for k in range(1, grids):
        pl.semaphore_signal(
            barrier, inc=1, device_id=device(lax.rem(g + k, grids), b, c), device_id_type=MESH
        )
    pl.semaphore_wait(barrier, plane - 1 + grids - 1)
    for load in loads:
        load.wait()

    def gather(k, total):
        hi, lo = split(window[depth * c + k])
        dims = ((1,), (1,))
        return total + mm(hi, rim_hi[k], dims) + mm(lo, rim_hi[k], dims) + mm(hi, rim_lo[k], dims)

    total = lax.fori_loop(0, extra, gather, sums_ref[...])
    hi, lo = split(total * scale_ref[...])
    first = extra + (half - extra) * c
    own = pl.ds(pl.multiple_of(b * nb, nb), nb)

    def row_copies(r):
        copies = []
        for k in sorted(range(1, bands), key=lambda v: -v):
            p = lax.rem(b + k, bands)
            copies.append(
                pltpu.make_async_remote_copy(
                    src_ref=y_ref.at[p, r],
                    dst_ref=yq_ref.at[r, own, :],
                    send_sem=a_sem.at[0, r, k - 1],
                    recv_sem=a_sem.at[1, r, k - 1],
                    device_id=device(g, p, c),
                    device_id_type=MESH,
                )
            )
        return copies

    def one(k, carry):
        for load in near_loads(k):
            load.wait()
        nonlocal_row = mm(hi, near_hi[k]) + mm(lo, near_hi[k]) + mm(hi, near_lo[k])
        row = base_ref[k] - STEP_SIZE * nonlocal_row
        for d in range(1, 7):
            pair = window[first + k + d] + window[first + k - d]
            row = row - (STEP_SIZE * KINETIC * STENCIL[d]) * pair
        for t in range(bands):
            y_ref[t, k] = row[:, t * width : (t + 1) * width]
        for copy in row_copies(k):
            copy.start()
        yq_ref[k, own, :] = y_ref[b, k]
        return carry

    lax.fori_loop(0, half, one, 0)
    s_ref[...] = jnp.zeros_like(s_ref)

    def add(r, carry):
        for copy in row_copies(r):
            copy.wait()
        hi, lo = split(yq_ref[r])
        cross = mm(hi, lo, ((1,), (1,)))
        s_ref[...] += mm(hi, hi, ((1,), (1,))) + (cross + cross.T)
        return carry

    lax.fori_loop(0, half, add, 0)
    part[...] = (s_ref[...] * scale).reshape(plane, share, size)

    copies = []
    for k in range(1, plane):
        p, where = plane_peer(k)
        copies.append(
            pltpu.make_async_remote_copy(
                src_ref=part.at[p],
                dst_ref=inbox.at[k - 1],
                send_sem=p_sem.at[0, k - 1],
                recv_sem=p_sem.at[1, k - 1],
                device_id=where,
                device_id_type=MESH,
            )
        )
        copies[-1].start()
    for copy in copies:
        copy.wait()
    total = part[me]
    for k in range(1, plane):
        total = total + inbox[k - 1]
    mine[...] = total
    zbox[g] = total
    copies = []
    for k in range(1, grids):
        copies.append(
            pltpu.make_async_remote_copy(
                src_ref=mine,
                dst_ref=zbox.at[g],
                send_sem=z_sem.at[0, k - 1],
                recv_sem=z_sem.at[1, k - 1],
                device_id=device(lax.rem(g + k, grids), b, c),
                device_id_type=MESH,
            )
        )
        copies[-1].start()
    for copy in copies:
        copy.wait()
    total = zbox[0]
    for k in range(1, grids):
        total = total + zbox[k]
    piece = pl.ds(pl.multiple_of(me * share, share), share)
    mine[...] = total
    copies = []
    for k in range(1, plane):
        copies.append(
            pltpu.make_async_remote_copy(
                src_ref=mine,
                dst_ref=s_ref.at[piece, :],
                send_sem=g_sem.at[0, k - 1],
                recv_sem=g_sem.at[1, k - 1],
                device_id=plane_peer(k)[1],
                device_id_type=MESH,
            )
        )
        copies[-1].start()
    s_ref[piece, :] = total
    for copy in copies:
        copy.wait()


def update_and_gram(halo, base, rows, sums, scale, dense, grids, bands, atoms, cells_total):
    extra, nb, cells = halo.shape
    half, depth = base.shape[0], rows.shape[0]
    projectors = sums.shape[1]
    size, width = bands * nb, cells // bands
    plane = bands * atoms
    share = size // plane
    vmem = pl.BlockSpec(memory_space=pltpu.VMEM)
    anywhere = pl.BlockSpec(memory_space=pl.ANY)
    return pl.pallas_call(
        functools.partial(gram_kernel, grids, bands, atoms, 1.0 / cells_total),
        out_shape=(
            jax.ShapeDtypeStruct((half, size, width), jnp.float32),
            jax.ShapeDtypeStruct((size, size), jnp.float32),
        ),
        in_specs=[anywhere, vmem, anywhere, vmem, vmem] + [anywhere] * 4,
        out_specs=(vmem, vmem),
        scratch_shapes=[
            pltpu.VMEM((depth + extra, nb, cells), jnp.float32),
            pltpu.VMEM((half, projectors, cells), jnp.bfloat16),
            pltpu.VMEM((half, projectors, cells), jnp.bfloat16),
            pltpu.VMEM((extra, projectors, cells), jnp.bfloat16),
            pltpu.VMEM((extra, projectors, cells), jnp.bfloat16),
            pltpu.VMEM((bands, half, nb, width), jnp.float32),
            pltpu.VMEM((plane, share, size), jnp.float32),
            pltpu.VMEM((plane - 1, share, size), jnp.float32),
            pltpu.VMEM((grids, share, size), jnp.float32),
            pltpu.VMEM((share, size), jnp.float32),
            pltpu.SemaphoreType.DMA((4,)),
            pltpu.SemaphoreType.DMA((2, half)),
            pltpu.SemaphoreType.DMA((2, half, bands - 1)),
            pltpu.SemaphoreType.DMA((2, plane - 1)),
            pltpu.SemaphoreType.DMA((2, grids - 1)),
            pltpu.SemaphoreType.DMA((2, plane - 1)),
        ],
        compiler_params=pltpu.CompilerParams(
            collective_id=0, has_side_effects=True, vmem_limit_bytes=60 << 20
        ),
    )(halo, base, rows, sums, scale, *dense)


def factor_kernel(step, s_ref, x_ref, work):
    size = s_ref.shape[0]
    work[:, :size] = s_ref[...]
    rows = lax.broadcasted_iota(jnp.int32, (size, size), 0)
    cols = lax.broadcasted_iota(jnp.int32, (size, size), 1)
    work[:, size:] = jnp.where(rows == cols, 1.0, 0.0)
    lanes = 2 * step
    row = lax.broadcasted_iota(jnp.int32, (8, lanes), 0)
    lane = lax.broadcasted_iota(jnp.int32, (8, lanes), 1)
    for k in range(size // step):
        lo, hi = k * step, (k + 1) * step
        tiles = []
        for t in range(step // 8):
            eye = jnp.where(lane[:, :step] == row[:, :step] + t * 8, 1.0, 0.0)
            tiles.append(
                jnp.concatenate([work[lo + t * 8 : lo + t * 8 + 8, lo:hi], eye], axis=1)
            )
        lines = []
        for j in range(step):
            t, r = j // 8, j % 8
            column = {
                u: jnp.broadcast_to(tiles[u][:, j : j + 1], (8, lanes)) for u in range(t, step // 8)
            }
            scaled = tiles[t][r : r + 1, :] * lax.rsqrt(column[t][r : r + 1, :])
            lines.append(scaled[:, step:])
            ratio = lax.rsqrt(column[t][r : r + 1, :])
            wide = jnp.broadcast_to(scaled * ratio, (8, lanes))
            tiles[t] = tiles[t] - jnp.where(row > r, column[t], 0.0) * wide
            for u in range(t + 1, step // 8):
                tiles[u] = tiles[u] - column[u] * wide
        inverse = jnp.concatenate(lines, axis=0)
        right = mm3(inverse, work[lo:hi, size : size + hi])
        x_ref[lo:hi, :hi] = right
        if hi < size:
            x_ref[lo:hi, hi:] = jnp.zeros((step, size - hi), jnp.float32)
            left = mm3(inverse, work[lo:hi, hi:size])
            work[hi:, hi:size] = work[hi:, hi:size] - mm3(left, left, ((0,), (0,)))
            work[hi:, size : size + hi] = work[hi:, size : size + hi] - mm3(left, right, ((0,), (0,)))


def inverse_factor(s, step):
    size = s.shape[0]
    vmem = pl.BlockSpec(memory_space=pltpu.VMEM)
    return pl.pallas_call(
        functools.partial(factor_kernel, step),
        out_shape=jax.ShapeDtypeStruct((size, size), jnp.float32),
        in_specs=[vmem],
        out_specs=vmem,
        scratch_shapes=[pltpu.VMEM((size, 2 * size), jnp.float32)],
    )(s)


def combine_kernel(bands, x_ref, yq_ref, o_ref, z, s_sem, r_sem):
    g, b, c = lax.axis_index("grid"), lax.axis_index("band"), lax.axis_index("atom")
    rows, size, width = yq_ref.shape
    nb = size // bands
    barrier = pltpu.get_barrier_semaphore()
    for k in range(1, bands):
        pl.semaphore_signal(
            barrier, inc=1, device_id=device(g, lax.rem(b + k, bands), c), device_id_type=MESH
        )
    pl.semaphore_wait(barrier, bands - 1)
    copies = []
    for r in range(rows):
        z[r] = mm3(x_ref[...], yq_ref[r])
        for k in range(1, bands):
            p = lax.rem(b + k, bands)
            copies.append(
                pltpu.make_async_remote_copy(
                    src_ref=z.at[r, pl.ds(pl.multiple_of(p * nb, nb), nb), :],
                    dst_ref=o_ref.at[b, r],
                    send_sem=s_sem.at[r, k - 1],
                    recv_sem=r_sem.at[r, k - 1],
                    device_id=device(g, p, c),
                    device_id_type=MESH,
                )
            )
            copies[-1].start()
    o_ref[b] = z[:, pl.ds(pl.multiple_of(b * nb, nb), nb), :]
    for copy in copies:
        copy.wait()


def combine_and_return(x, yq, bands):
    rows, size, width = yq.shape
    vmem = pl.BlockSpec(memory_space=pltpu.VMEM)
    return pl.pallas_call(
        functools.partial(combine_kernel, bands),
        out_shape=jax.ShapeDtypeStruct((bands, rows, size // bands, width), jnp.float32),
        in_specs=[vmem, vmem],
        out_specs=vmem,
        scratch_shapes=[
            pltpu.VMEM((rows, size, width), jnp.float32),
            pltpu.SemaphoreType.DMA((rows, bands - 1)),
            pltpu.SemaphoreType.DMA((rows, bands - 1)),
        ],
        compiler_params=pltpu.CompilerParams(
            collective_id=1, has_side_effects=True, vmem_limit_bytes=56 << 20
        ),
    )(x, yq)


def plane_kernel(core_rows, rows_ref, potential_ref, base_ref, weights):
    depth, nb, cells = rows_ref.shape
    half = base_ref.shape[0]
    tile = weights.shape[1]
    reach = tile // CY
    shape = weights.shape
    source = lax.broadcasted_iota(jnp.int32, shape, 0) - tile
    target = lax.broadcasted_iota(jnp.int32, shape, 1)
    dx = jnp.abs((source + tile) // CY - reach - target // CY)
    dy = jnp.abs((source + tile) % CY - target % CY)
    value = jnp.zeros(shape, jnp.float32)
    for k in range(1, 7):
        hit = ((dx == k) & (dy == 0)) | ((dx == 0) & (dy == k))
        value = jnp.where(hit, STENCIL[k], value)
    weights[...] = value
    first = lax.axis_index("atom") * core_rows

    def one(k, carry):
        for t in range(cells // tile):
            here = slice(t * tile, (t + 1) * tile)
            low, high = max(t - 1, 0), min(t + 2, cells // tile)
            field = rows_ref[first + k, :, low * tile : high * tile]
            band = weights[(low - t + 1) * tile : (high - t + 1) * tile, :]
            plane = mm3(field, band)
            centre = rows_ref[first + k, :, here]
            applied = KINETIC * (3.0 * STENCIL[0] * centre + plane)
            applied = applied + potential_ref[pl.ds(k, 1), here] * centre
            base_ref[k, :, here] = centre - STEP_SIZE * applied
        return carry

    lax.fori_loop(0, half, one, 0)


def plane_part(rows, potential):
    depth, nb, cells = rows.shape
    half = potential.shape[0]
    vmem = pl.BlockSpec(memory_space=pltpu.VMEM)
    tile = 8 * CY
    return pl.pallas_call(
        functools.partial(plane_kernel, half),
        out_shape=jax.ShapeDtypeStruct((half, nb, cells), jnp.float32),
        in_specs=[vmem, vmem],
        out_specs=vmem,
        scratch_shapes=[pltpu.VMEM((3 * tile, tile), jnp.float32)],
        compiler_params=pltpu.CompilerParams(vmem_limit_bytes=56 << 20),
        cost_estimate=pl.CostEstimate(
            flops=12 * half * nb * cells * tile, bytes_accessed=40 * nb * half * cells, transcendentals=0
        ),
    )(rows, potential)


def dense_kernel(
    extra, edge, table_ref, own_ref, other_ref, rows_ref, sums_ref, near_hi, near_lo, rim_hi, rim_lo,
    dense, cubes,
):
    core = lax.axis_index("atom")
    half, projectors, cells = near_hi.shape
    depth = rows_ref.shape[0]
    window = depth + extra
    atoms = table_ref.shape[1]
    each = projectors // atoms
    count = own_ref.shape[0]
    flat, wide = edge * edge, edge * CY

    def clear(w, carry):
        dense[w] = jnp.zeros(dense.shape[1:], jnp.float32)
        return carry

    lax.fori_loop(0, window, clear, 0)
    point = lax.broadcasted_iota(jnp.int32, (flat, wide), 0)
    place = lax.broadcasted_iota(jnp.int32, (flat, wide), 1)
    spread = (point // edge == place // CY) & (point % edge == place % CY)
    spread = jnp.where(spread, 1.0, 0.0).astype(jnp.bfloat16)
    for e in range(edge):
        for values, low in ((own_ref, 0), (other_ref, count)):
            hi, lo = split(values[:count, e * flat : (e + 1) * flat])
            cubes[e, low : low + count, :] = mm(hi, spread) + mm(lo, spread)
    pair = 8 // each

    def build(p, carry):
        rows = pl.ds(pl.multiple_of(p * 8, 8), 8)
        group = dense.at[:, rows, :]
        for h in range(pair):
            atom = p * pair + h

            @pl.when(table_ref[2, atom] > 0)
            def _():
                lane = table_ref[1, atom]
                start = table_ref[0, atom]
                cube = cubes[:, rows, :].reshape(edge * 8, wide)
                cube = jnp.concatenate([cube, jnp.zeros((edge * 8, 128), jnp.float32)], axis=1)
                moved = pltpu.roll(cube, lax.rem(lane, 128), 1).reshape(edge, 8, wide + 128)
                at = pl.ds(pl.multiple_of(lane // 128 * 128, 128), wide + 128)
                for e in range(edge):
                    group[start + e, h * each : (h + 1) * each, at] = moved[
                        e, h * each : (h + 1) * each, :
                    ]

        return carry

    lax.fori_loop(0, atoms // pair, build, 0)
    ahead = extra * (1 - core)
    sums_ref[...] = jnp.zeros_like(sums_ref)

    def gather(r, carry):
        sums_ref[...] += mm3(rows_ref[r], dense[r + ahead, :, :cells], ((1,), (1,)))
        return carry

    lax.fori_loop(0, depth, gather, 0)
    own = extra + (half - extra) * core

    def keep_near(k, carry):
        near_hi[k], near_lo[k] = split(dense[own + k, :, :cells])
        return carry

    def keep_rim(k, carry):
        rim_hi[k], rim_lo[k] = split(dense[depth * core + k, :, :cells])
        return carry

    lax.fori_loop(0, half, keep_near, 0)
    lax.fori_loop(0, extra, keep_rim, 0)


def dense_projectors(table, ordered, other, rows, half, extra, each, edge):
    depth, nb, cells = rows.shape
    projectors = table.shape[1] * each
    vmem = pl.BlockSpec(memory_space=pltpu.VMEM)
    near = jax.ShapeDtypeStruct((half, projectors, cells), jnp.bfloat16)
    rim = jax.ShapeDtypeStruct((extra, projectors, cells), jnp.bfloat16)
    return pl.pallas_call(
        functools.partial(dense_kernel, extra, edge),
        out_shape=(jax.ShapeDtypeStruct((nb, projectors), jnp.float32), near, near, rim, rim),
        in_specs=[pl.BlockSpec(memory_space=pltpu.SMEM), vmem, vmem, vmem],
        out_specs=(vmem,) * 5,
        scratch_shapes=[
            pltpu.VMEM((depth + extra, projectors, cells + 128), jnp.float32),
            pltpu.VMEM((edge, projectors, edge * CY), jnp.float32),
        ],
        compiler_params=pltpu.CompilerParams(vmem_limit_bytes=60 << 20),
        cost_estimate=pl.CostEstimate(
            flops=6 * depth * nb * cells * projectors,
            bytes_accessed=4 * (depth + half) * projectors * cells,
            transcendentals=0,
        ),
    )(table, ordered, other, rows)


def in_cube_order(projectors, sphere_index, edge, plane_cells):
    cell = lax.iota(jnp.int32, edge * edge * edge)
    offset = cell // (edge * edge) * plane_cells + cell // edge % edge * CY + cell % edge
    first = jnp.min(sphere_index, axis=1, keepdims=True)
    ordered = jnp.all(sphere_index == first + offset[None])

    def arrange(values):
        order = jnp.argsort(sphere_index, axis=1)
        return jnp.take_along_axis(values, order[:, None, :], axis=2)

    return lax.cond(ordered, lambda values: values, arrange, projectors), first[:, 0]


def body(psi, potential, projectors, strength, sphere_index, atom_count):
    band_rows, depth, plane_cells = psi.shape
    groups, grids, bands = (lax.axis_size(name) for name in ("atom", "grid", "band"))
    core = lax.axis_index("atom")
    half = depth // groups
    atom_slots, each, points = projectors.shape
    edge = round(points ** (1 / 3))
    extra = edge - 1
    route = []
    for i in range(grids):
        route.append((i * groups + 1, (i + 1) % grids * groups))
        route.append((i * groups, (i - 1) % grids * groups + 1))

    edge_rows = lax.dynamic_slice_in_dim(psi, core * (depth - extra), extra, 1).transpose(1, 0, 2)
    edge_rows, psi, projectors, sphere_index = lax.optimization_barrier(
        (edge_rows, psi, projectors, sphere_index)
    )
    halo = lax.ppermute(edge_rows, ("grid", "atom"), route)
    ordered, first = in_cube_order(projectors, sphere_index, edge, plane_cells)
    alive_mask = (lax.iota(jnp.int32, atom_slots) < atom_count[0]).astype(jnp.float32)
    scaled = strength * alive_mask[:, None] / math.sqrt(points)
    count = atom_slots * each
    lines = -(-count // points)
    scaled_line = jnp.pad(scaled.reshape(-1), (0, lines * points - count)).reshape(lines, points)
    first_line = jnp.pad(first.astype(jnp.float32), (0, points - atom_slots))[None]
    sent = jnp.concatenate([ordered.reshape(count, points), scaled_line, first_line], axis=0)
    got = lax.ppermute(sent, ("grid", "atom"), route)
    rows = psi.transpose(1, 0, 2)
    base = plane_part(rows, potential)
    other_first = got[-1, :atom_slots].astype(jnp.int32)
    other_scaled = got[count : count + lines].reshape(-1)[:count]
    bottom = jnp.concatenate(
        [first // plane_cells - 6, other_first // plane_cells - 6 + depth * (2 * core - 1)]
    )
    lane = jnp.concatenate([first % plane_cells, other_first % plane_cells])
    touches = (bottom < half * (core + 1)) & (bottom + edge > half * core)
    start = jnp.clip(bottom + extra * (1 - core), 0, depth + extra - edge)
    table = jnp.stack([start, lane, touches.astype(jnp.int32)])
    flat = ordered.reshape(count, points)
    dense = dense_projectors(table, flat, got, rows, half, extra, each, edge)
    scale = jnp.concatenate([scaled.reshape(-1), other_scaled])[None]
    cells_total = grids * depth * plane_cells
    gathered, intersection_matrix = update_and_gram(
        halo, base, rows, dense[0], scale, dense[1:], grids, bands, groups, cells_total
    )
    inverse = inverse_factor(intersection_matrix, band_rows)
    pieces = combine_and_return(inverse, gathered, bands)
    return pieces.transpose(2, 1, 0, 3).reshape(band_rows, half, plane_cells)


def solution(mesh):
    in_specs = (
        P("band", "grid", None),
        P(("grid", "atom"), None),
        P("grid", None, None),
        P("grid", None),
        P("grid", None),
        P("grid"),
    )
    out_specs = P("band", ("grid", "atom"), None)
    return jax.shard_map(body, mesh=mesh, in_specs=in_specs, out_specs=out_specs, check_vma=False)
```

```python
import functools
import math

import jax
import jax.numpy as jnp
from jax import lax
from jax.experimental import pallas as pl
from jax.experimental.pallas import tpu as pltpu
from jax.sharding import PartitionSpec as P

CY = 32


STENCIL = (
    -5369.0 / 1800.0,
    12.0 / 7.0,
    -15.0 / 56.0,
    10.0 / 189.0,
    -1.0 / 112.0,
    2.0 / 1925.0,
    -1.0 / 16632.0,
)
KINETIC = -0.5 * 4.0
STEP_SIZE = 0.05
HIGHEST = lax.Precision.HIGHEST
MESH = pl.DeviceIdType.MESH


def split(x):
    hi = x.astype(jnp.bfloat16)
    return hi, (x - hi.astype(jnp.float32)).astype(jnp.bfloat16)


def mm(a, b, dims=((1,), (0,))):
    return lax.dot_general(a, b, (dims, ((), ())), preferred_element_type=jnp.float32)


def mm3(a, b, dims=((1,), (0,))):
    ah, al = split(a)
    bh, bl = split(b)
    return mm(ah, bh, dims) + (mm(ah, bl, dims) + mm(al, bh, dims))


def device(grid, band, atom):
    return {"grid": grid, "band": band, "atom": atom}


def gram_kernel(
    grids, bands, atoms, scale, halo_ref, base_ref, rows_ref, sums_ref, scale_ref, near_hi_ref,
    near_lo_ref, rim_hi_ref, rim_lo_ref, yq_ref, s_ref, window, near_hi, near_lo, rim_hi, rim_lo,
    y_ref, part, inbox, zbox, mine, d_sem, n_sem, a_sem, p_sem, z_sem, g_sem,
):
    g, b, c = lax.axis_index("grid"), lax.axis_index("band"), lax.axis_index("atom")
    plane = bands * atoms
    me = b * atoms + c
    half, nb, width = y_ref.shape[1:]
    size = s_ref.shape[0]
    share = size // plane
    extra, depth = rim_hi.shape[0], window.shape[0] - rim_hi.shape[0]

    loads = [
        pltpu.make_async_copy(rim_hi_ref, rim_hi, d_sem.at[0]),
        pltpu.make_async_copy(rim_lo_ref, rim_lo, d_sem.at[1]),
        pltpu.make_async_copy(halo_ref, window.at[pl.ds(depth * c, extra)], d_sem.at[2]),
        pltpu.make_async_copy(rows_ref, window.at[pl.ds(extra * (1 - c), depth)], d_sem.at[3]),
    ]
    for load in loads:
        load.start()

    def near_loads(k):
        return (
            pltpu.make_async_copy(near_hi_ref.at[k], near_hi.at[k], n_sem.at[0, k]),
            pltpu.make_async_copy(near_lo_ref.at[k], near_lo.at[k], n_sem.at[1, k]),
        )

    def start_near(k, carry):
        for load in near_loads(k):
            load.start()
        return carry

    lax.fori_loop(0, half, start_near, 0)

    def plane_peer(k):
        p = lax.rem(me + k, plane)
        return p, device(g, p // atoms, lax.rem(p, atoms))

    barrier = pltpu.get_barrier_semaphore()
    for k in range(1, plane):
        pl.semaphore_signal(barrier, inc=1, device_id=plane_peer(k)[1], device_id_type=MESH)
    for k in range(1, grids):
        pl.semaphore_signal(
            barrier, inc=1, device_id=device(lax.rem(g + k, grids), b, c), device_id_type=MESH
        )
    pl.semaphore_wait(barrier, plane - 1 + grids - 1)
    for load in loads:
        load.wait()

    def gather(k, total):
        hi, lo = split(window[depth * c + k])
        dims = ((1,), (1,))
        return total + mm(hi, rim_hi[k], dims) + mm(lo, rim_hi[k], dims) + mm(hi, rim_lo[k], dims)

    total = lax.fori_loop(0, extra, gather, sums_ref[...])
    hi, lo = split(total * scale_ref[...])
    first = extra + (half - extra) * c
    own = pl.ds(pl.multiple_of(b * nb, nb), nb)

    def row_copies(r):
        copies = []
        for k in sorted(range(1, bands), key=lambda v: -v):
            p = lax.rem(b + k, bands)
            copies.append(
                pltpu.make_async_remote_copy(
                    src_ref=y_ref.at[p, r],
                    dst_ref=yq_ref.at[r, own, :],
                    send_sem=a_sem.at[0, r, k - 1],
                    recv_sem=a_sem.at[1, r, k - 1],
                    device_id=device(g, p, c),
                    device_id_type=MESH,
                )
            )
        return copies

    def one(k, carry):
        for load in near_loads(k):
            load.wait()
        nonlocal_row = mm(hi, near_hi[k]) + mm(lo, near_hi[k]) + mm(hi, near_lo[k])
        row = base_ref[k] - STEP_SIZE * nonlocal_row
        for d in range(1, 7):
            pair = window[first + k + d] + window[first + k - d]
            row = row - (STEP_SIZE * KINETIC * STENCIL[d]) * pair
        for t in range(bands):
            y_ref[t, k] = row[:, t * width : (t + 1) * width]
        for copy in row_copies(k):
            copy.start()
        yq_ref[k, own, :] = y_ref[b, k]
        return carry

    lax.fori_loop(0, half, one, 0)
    s_ref[...] = jnp.zeros_like(s_ref)

    def add(r, carry):
        for copy in row_copies(r):
            copy.wait()
        hi, lo = split(yq_ref[r])
        cross = mm(hi, lo, ((1,), (1,)))
        s_ref[...] += mm(hi, hi, ((1,), (1,))) + (cross + cross.T)
        return carry

    lax.fori_loop(0, half, add, 0)
    part[...] = (s_ref[...] * scale).reshape(plane, share, size)

    copies = []
    for k in range(1, plane):
        p, where = plane_peer(k)
        copies.append(
            pltpu.make_async_remote_copy(
                src_ref=part.at[p],
                dst_ref=inbox.at[k - 1],
                send_sem=p_sem.at[0, k - 1],
                recv_sem=p_sem.at[1, k - 1],
                device_id=where,
                device_id_type=MESH,
            )
        )
        copies[-1].start()
    for copy in copies:
        copy.wait()
    total = part[me]
    for k in range(1, plane):
        total = total + inbox[k - 1]
    mine[...] = total
    zbox[g] = total
    copies = []
    for k in range(1, grids):
        copies.append(
            pltpu.make_async_remote_copy(
                src_ref=mine,
                dst_ref=zbox.at[g],
                send_sem=z_sem.at[0, k - 1],
                recv_sem=z_sem.at[1, k - 1],
                device_id=device(lax.rem(g + k, grids), b, c),
                device_id_type=MESH,
            )
        )
        copies[-1].start()
    for copy in copies:
        copy.wait()
    total = zbox[0]
    for k in range(1, grids):
        total = total + zbox[k]
    piece = pl.ds(pl.multiple_of(me * share, share), share)
    mine[...] = total
    copies = []
    for k in range(1, plane):
        copies.append(
            pltpu.make_async_remote_copy(
                src_ref=mine,
                dst_ref=s_ref.at[piece, :],
                send_sem=g_sem.at[0, k - 1],
                recv_sem=g_sem.at[1, k - 1],
                device_id=plane_peer(k)[1],
                device_id_type=MESH,
            )
        )
        copies[-1].start()
    s_ref[piece, :] = total
    for copy in copies:
        copy.wait()


def update_and_gram(halo, base, rows, sums, scale, dense, grids, bands, atoms, cells_total):
    extra, nb, cells = halo.shape
    half, depth = base.shape[0], rows.shape[0]
    projectors = sums.shape[1]
    size, width = bands * nb, cells // bands
    plane = bands * atoms
    share = size // plane
    vmem = pl.BlockSpec(memory_space=pltpu.VMEM)
    anywhere = pl.BlockSpec(memory_space=pl.ANY)
    return pl.pallas_call(
        functools.partial(gram_kernel, grids, bands, atoms, 1.0 / cells_total),
        out_shape=(
            jax.ShapeDtypeStruct((half, size, width), jnp.float32),
            jax.ShapeDtypeStruct((size, size), jnp.float32),
        ),
        in_specs=[anywhere, vmem, anywhere, vmem, vmem] + [anywhere] * 4,
        out_specs=(vmem, vmem),
        scratch_shapes=[
            pltpu.VMEM((depth + extra, nb, cells), jnp.float32),
            pltpu.VMEM((half, projectors, cells), jnp.bfloat16),
            pltpu.VMEM((half, projectors, cells), jnp.bfloat16),
            pltpu.VMEM((extra, projectors, cells), jnp.bfloat16),
            pltpu.VMEM((extra, projectors, cells), jnp.bfloat16),
            pltpu.VMEM((bands, half, nb, width), jnp.float32),
            pltpu.VMEM((plane, share, size), jnp.float32),
            pltpu.VMEM((plane - 1, share, size), jnp.float32),
            pltpu.VMEM((grids, share, size), jnp.float32),
            pltpu.VMEM((share, size), jnp.float32),
            pltpu.SemaphoreType.DMA((4,)),
            pltpu.SemaphoreType.DMA((2, half)),
            pltpu.SemaphoreType.DMA((2, half, bands - 1)),
            pltpu.SemaphoreType.DMA((2, plane - 1)),
            pltpu.SemaphoreType.DMA((2, grids - 1)),
            pltpu.SemaphoreType.DMA((2, plane - 1)),
        ],
        compiler_params=pltpu.CompilerParams(
            collective_id=0, has_side_effects=True, vmem_limit_bytes=60 << 20
        ),
    )(halo, base, rows, sums, scale, *dense)


def factor_kernel(step, s_ref, x_ref, work):
    size = s_ref.shape[0]
    work[:, :size] = s_ref[...]
    rows = lax.broadcasted_iota(jnp.int32, (size, size), 0)
    cols = lax.broadcasted_iota(jnp.int32, (size, size), 1)
    work[:, size:] = jnp.where(rows == cols, 1.0, 0.0)
    lanes = 2 * step
    row = lax.broadcasted_iota(jnp.int32, (8, lanes), 0)
    lane = lax.broadcasted_iota(jnp.int32, (8, lanes), 1)
    for k in range(size // step):
        lo, hi = k * step, (k + 1) * step
        tiles = []
        for t in range(step // 8):
            eye = jnp.where(lane[:, :step] == row[:, :step] + t * 8, 1.0, 0.0)
            tiles.append(
                jnp.concatenate([work[lo + t * 8 : lo + t * 8 + 8, lo:hi], eye], axis=1)
            )
        lines = []
        for j in range(step):
            t, r = j // 8, j % 8
            column = {
                u: jnp.broadcast_to(tiles[u][:, j : j + 1], (8, lanes)) for u in range(t, step // 8)
            }
            scaled = tiles[t][r : r + 1, :] * lax.rsqrt(column[t][r : r + 1, :])
            lines.append(scaled[:, step:])
            ratio = lax.rsqrt(column[t][r : r + 1, :])
            wide = jnp.broadcast_to(scaled * ratio, (8, lanes))
            tiles[t] = tiles[t] - jnp.where(row > r, column[t], 0.0) * wide
            for u in range(t + 1, step // 8):
                tiles[u] = tiles[u] - column[u] * wide
        inverse = jnp.concatenate(lines, axis=0)
        right = mm3(inverse, work[lo:hi, size : size + hi])
        x_ref[lo:hi, :hi] = right
        if hi < size:
            x_ref[lo:hi, hi:] = jnp.zeros((step, size - hi), jnp.float32)
            left = mm3(inverse, work[lo:hi, hi:size])
            work[hi:, hi:size] = work[hi:, hi:size] - mm3(left, left, ((0,), (0,)))
            work[hi:, size : size + hi] = work[hi:, size : size + hi] - mm3(left, right, ((0,), (0,)))


def inverse_factor(s, step):
    size = s.shape[0]
    vmem = pl.BlockSpec(memory_space=pltpu.VMEM)
    return pl.pallas_call(
        functools.partial(factor_kernel, step),
        out_shape=jax.ShapeDtypeStruct((size, size), jnp.float32),
        in_specs=[vmem],
        out_specs=vmem,
        scratch_shapes=[pltpu.VMEM((size, 2 * size), jnp.float32)],
    )(s)


def combine_kernel(bands, x_ref, yq_ref, o_ref, z, s_sem, r_sem):
    g, b, c = lax.axis_index("grid"), lax.axis_index("band"), lax.axis_index("atom")
    rows, size, width = yq_ref.shape
    nb = size // bands
    barrier = pltpu.get_barrier_semaphore()
    for k in range(1, bands):
        pl.semaphore_signal(
            barrier, inc=1, device_id=device(g, lax.rem(b + k, bands), c), device_id_type=MESH
        )
    pl.semaphore_wait(barrier, bands - 1)
    copies = []
    for r in range(rows):
        z[r] = mm3(x_ref[...], yq_ref[r])
        for k in range(1, bands):
            p = lax.rem(b + k, bands)
            copies.append(
                pltpu.make_async_remote_copy(
                    src_ref=z.at[r, pl.ds(pl.multiple_of(p * nb, nb), nb), :],
                    dst_ref=o_ref.at[b, r],
                    send_sem=s_sem.at[r, k - 1],
                    recv_sem=r_sem.at[r, k - 1],
                    device_id=device(g, p, c),
                    device_id_type=MESH,
                )
            )
            copies[-1].start()
    o_ref[b] = z[:, pl.ds(pl.multiple_of(b * nb, nb), nb), :]
    for copy in copies:
        copy.wait()


def combine_and_return(x, yq, bands):
    rows, size, width = yq.shape
    vmem = pl.BlockSpec(memory_space=pltpu.VMEM)
    return pl.pallas_call(
        functools.partial(combine_kernel, bands),
        out_shape=jax.ShapeDtypeStruct((bands, rows, size // bands, width), jnp.float32),
        in_specs=[vmem, vmem],
        out_specs=vmem,
        scratch_shapes=[
            pltpu.VMEM((rows, size, width), jnp.float32),
            pltpu.SemaphoreType.DMA((rows, bands - 1)),
            pltpu.SemaphoreType.DMA((rows, bands - 1)),
        ],
        compiler_params=pltpu.CompilerParams(
            collective_id=1, has_side_effects=True, vmem_limit_bytes=56 << 20
        ),
    )(x, yq)


def plane_kernel(core_rows, rows_ref, potential_ref, base_ref, weights):
    depth, nb, cells = rows_ref.shape
    half = base_ref.shape[0]
    tile = weights.shape[1]
    reach = tile // CY
    shape = weights.shape
    source = lax.broadcasted_iota(jnp.int32, shape, 0) - tile
    target = lax.broadcasted_iota(jnp.int32, shape, 1)
    dx = jnp.abs((source + tile) // CY - reach - target // CY)
    dy = jnp.abs((source + tile) % CY - target % CY)
    value = jnp.zeros(shape, jnp.float32)
    for k in range(1, 7):
        hit = ((dx == k) & (dy == 0)) | ((dx == 0) & (dy == k))
        value = jnp.where(hit, STENCIL[k], value)
    weights[...] = value
    first = lax.axis_index("atom") * core_rows

    def one(k, carry):
        for t in range(cells // tile):
            here = slice(t * tile, (t + 1) * tile)
            low, high = max(t - 1, 0), min(t + 2, cells // tile)
            field = rows_ref[first + k, :, low * tile : high * tile]
            band = weights[(low - t + 1) * tile : (high - t + 1) * tile, :]
            plane = mm3(field, band)
            centre = rows_ref[first + k, :, here]
            applied = KINETIC * (3.0 * STENCIL[0] * centre + plane)
            applied = applied + potential_ref[pl.ds(k, 1), here] * centre
            base_ref[k, :, here] = centre - STEP_SIZE * applied
        return carry

    lax.fori_loop(0, half, one, 0)


def plane_part(rows, potential):
    depth, nb, cells = rows.shape
    half = potential.shape[0]
    vmem = pl.BlockSpec(memory_space=pltpu.VMEM)
    tile = 8 * CY
    return pl.pallas_call(
        functools.partial(plane_kernel, half),
        out_shape=jax.ShapeDtypeStruct((half, nb, cells), jnp.float32),
        in_specs=[vmem, vmem],
        out_specs=vmem,
        scratch_shapes=[pltpu.VMEM((3 * tile, tile), jnp.float32)],
        compiler_params=pltpu.CompilerParams(vmem_limit_bytes=56 << 20),
        cost_estimate=pl.CostEstimate(
            flops=12 * half * nb * cells * tile, bytes_accessed=40 * nb * half * cells, transcendentals=0
        ),
    )(rows, potential)


def dense_kernel(
    extra, edge, table_ref, own_ref, other_ref, rows_ref, sums_ref, near_hi, near_lo, rim_hi, rim_lo,
    dense, cubes,
):
    core = lax.axis_index("atom")
    half, projectors, cells = near_hi.shape
    depth = rows_ref.shape[0]
    window = depth + extra
    atoms = table_ref.shape[1]
    each = projectors // atoms
    count = own_ref.shape[0]
    flat, wide = edge * edge, edge * CY

    def clear(w, carry):
        dense[w] = jnp.zeros(dense.shape[1:], jnp.float32)
        return carry

    lax.fori_loop(0, window, clear, 0)
    point = lax.broadcasted_iota(jnp.int32, (flat, wide), 0)
    place = lax.broadcasted_iota(jnp.int32, (flat, wide), 1)
    spread = (point // edge == place // CY) & (point % edge == place % CY)
    spread = jnp.where(spread, 1.0, 0.0).astype(jnp.bfloat16)
    for e in range(edge):
        for values, low in ((own_ref, 0), (other_ref, count)):
            hi, lo = split(values[:count, e * flat : (e + 1) * flat])
            cubes[e, low : low + count, :] = mm(hi, spread) + mm(lo, spread)
    pair = 8 // each

    def build(p, carry):
        rows = pl.ds(pl.multiple_of(p * 8, 8), 8)
        group = dense.at[:, rows, :]
        for h in range(pair):
            atom = p * pair + h

            @pl.when(table_ref[2, atom] > 0)
            def _():
                lane = table_ref[1, atom]
                start = table_ref[0, atom]
                cube = cubes[:, rows, :].reshape(edge * 8, wide)
                cube = jnp.concatenate([cube, jnp.zeros((edge * 8, 128), jnp.float32)], axis=1)
                moved = pltpu.roll(cube, lax.rem(lane, 128), 1).reshape(edge, 8, wide + 128)
                at = pl.ds(pl.multiple_of(lane // 128 * 128, 128), wide + 128)
                for e in range(edge):
                    group[start + e, h * each : (h + 1) * each, at] = moved[
                        e, h * each : (h + 1) * each, :
                    ]

        return carry

    lax.fori_loop(0, atoms // pair, build, 0)
    ahead = extra * (1 - core)
    sums_ref[...] = jnp.zeros_like(sums_ref)

    def gather(r, carry):
        sums_ref[...] += mm3(rows_ref[r], dense[r + ahead, :, :cells], ((1,), (1,)))
        return carry

    lax.fori_loop(0, depth, gather, 0)
    own = extra + (half - extra) * core

    def keep_near(k, carry):
        near_hi[k], near_lo[k] = split(dense[own + k, :, :cells])
        return carry

    def keep_rim(k, carry):
        rim_hi[k], rim_lo[k] = split(dense[depth * core + k, :, :cells])
        return carry

    lax.fori_loop(0, half, keep_near, 0)
    lax.fori_loop(0, extra, keep_rim, 0)


def dense_projectors(table, ordered, other, rows, half, extra, each, edge):
    depth, nb, cells = rows.shape
    projectors = table.shape[1] * each
    vmem = pl.BlockSpec(memory_space=pltpu.VMEM)
    near = jax.ShapeDtypeStruct((half, projectors, cells), jnp.bfloat16)
    rim = jax.ShapeDtypeStruct((extra, projectors, cells), jnp.bfloat16)
    return pl.pallas_call(
        functools.partial(dense_kernel, extra, edge),
        out_shape=(jax.ShapeDtypeStruct((nb, projectors), jnp.float32), near, near, rim, rim),
        in_specs=[pl.BlockSpec(memory_space=pltpu.SMEM), vmem, vmem, vmem],
        out_specs=(vmem,) * 5,
        scratch_shapes=[
            pltpu.VMEM((depth + extra, projectors, cells + 128), jnp.float32),
            pltpu.VMEM((edge, projectors, edge * CY), jnp.float32),
        ],
        compiler_params=pltpu.CompilerParams(vmem_limit_bytes=60 << 20),
        cost_estimate=pl.CostEstimate(
            flops=6 * depth * nb * cells * projectors,
            bytes_accessed=4 * (depth + half) * projectors * cells,
            transcendentals=0,
        ),
    )(table, ordered, other, rows)


def in_cube_order(projectors, sphere_index, edge, plane_cells):
    cell = lax.iota(jnp.int32, edge * edge * edge)
    offset = cell // (edge * edge) * plane_cells + cell // edge % edge * CY + cell % edge
    first = jnp.min(sphere_index, axis=1, keepdims=True)
    ordered = jnp.all(sphere_index == first + offset[None])

    def arrange(values):
        step = sphere_index - first
        x, y = step % plane_cells // CY, step % CY
        rank = step // plane_cells * (edge * edge) + x * edge + y
        here = (rank[:, :, None] == lax.iota(jnp.int32, edge**3)).astype(jnp.float32)
        return jnp.einsum("ais,aso->aio", values, here, precision=HIGHEST)

    return lax.cond(ordered, lambda values: values, arrange, projectors), first[:, 0]


def body(psi, potential, projectors, strength, sphere_index, atom_count):
    band_rows, depth, plane_cells = psi.shape
    groups, grids, bands = (lax.axis_size(name) for name in ("atom", "grid", "band"))
    core = lax.axis_index("atom")
    half = depth // groups
    atom_slots, each, points = projectors.shape
    edge = round(points ** (1 / 3))
    extra = edge - 1
    route = []
    for i in range(grids):
        route.append((i * groups + 1, (i + 1) % grids * groups))
        route.append((i * groups, (i - 1) % grids * groups + 1))

    ordered, first = in_cube_order(projectors, sphere_index, edge, plane_cells)
    alive_mask = (lax.iota(jnp.int32, atom_slots) < atom_count[0]).astype(jnp.float32)
    scaled = strength * alive_mask[:, None] / math.sqrt(points)
    count = atom_slots * each
    lines = -(-count // points)
    scaled_line = jnp.pad(scaled.reshape(-1), (0, lines * points - count)).reshape(lines, points)
    first_line = jnp.pad(first.astype(jnp.float32), (0, points - atom_slots))[None]
    sent = jnp.concatenate([ordered.reshape(count, points), scaled_line, first_line], axis=0)
    got = lax.ppermute(sent, ("grid", "atom"), route)
    rows = psi.transpose(1, 0, 2)
    edge_rows = lax.dynamic_slice_in_dim(rows, core * (depth - extra), extra, 0)
    got, edge_rows = lax.optimization_barrier((got, edge_rows))
    halo = lax.ppermute(edge_rows, ("grid", "atom"), route)
    base = plane_part(rows, potential)
    other_first = got[-1, :atom_slots].astype(jnp.int32)
    other_scaled = got[count : count + lines].reshape(-1)[:count]
    bottom = jnp.concatenate(
        [first // plane_cells - 6, other_first // plane_cells - 6 + depth * (2 * core - 1)]
    )
    lane = jnp.concatenate([first % plane_cells, other_first % plane_cells])
    touches = (bottom < half * (core + 1)) & (bottom + edge > half * core)
    start = jnp.clip(bottom + extra * (1 - core), 0, depth + extra - edge)
    table = jnp.stack([start, lane, touches.astype(jnp.int32)])
    flat = ordered.reshape(count, points)
    dense = dense_projectors(table, flat, got, rows, half, extra, each, edge)
    scale = jnp.concatenate([scaled.reshape(-1), other_scaled])[None]
    cells_total = grids * depth * plane_cells
    gathered, intersection_matrix = update_and_gram(
        halo, base, rows, dense[0], scale, dense[1:], grids, bands, groups, cells_total
    )
    inverse = inverse_factor(intersection_matrix, band_rows)
    pieces = combine_and_return(inverse, gathered, bands)
    return pieces.transpose(2, 1, 0, 3).reshape(band_rows, half, plane_cells)


def solution(mesh):
    in_specs = (
        P("band", "grid", None),
        P(("grid", "atom"), None),
        P("grid", None, None),
        P("grid", None),
        P("grid", None),
        P("grid"),
    )
    out_specs = P("band", ("grid", "atom"), None)
    return jax.shard_map(body, mesh=mesh, in_specs=in_specs, out_specs=out_specs, check_vma=False)
```
